256 devices in a mesh: band: 64 (over z, y, core), field: 4 (over x).
Axes of the slice: x: 4, y: 4, z: 8, core: 2. Of those that a mesh axis runs over, the one named last changes fastest.
Arguments:
- right_side: float32 [640, 2, 4, 12, 640], P('band', None, 'field'), may hold values from -40 to 40
- legendre: bfloat16 [640, 640, 640], P('band'), may hold values from -0.25 to 0.25
- wave_map: int32 [640], replicated, may hold values from 0 to 639, as said below
- obs_weight: float32 [640, 1280], P('band'), may hold values from 0.2 to 5
Outputs:
- solution: float32 [640, 2, 4, 12, 640], P('band', None, 'field')
- residual: float32 [640, 2, 4, 12, 640], P('band', None, 'field')
The draws below stay inside these ranges and needn't reach their ends.
Inputs may be any that keep to these rules, and one draw needn't show every extreme that they name: A permutation of 0 to 639; wave_map[s] lies in the same aligned block of 20 values as 639-s.
All inputs are finite; a program needn't handle non-finite values.
Results may differ from the reference program's by a relative error of at most 0.03.
Values may be sent and summed in bfloat16 or wider, within the bound.
A program may use at most 128 MiB of HBM per device.

```python
import math
import jax
import jax.numpy as jnp
from jax import lax

MW = 640
NLAT = 640
NLON = 1280
FIELDS = 4
LEV = 12
ITERS = 3


def draw_right_side(key, part):
    first_key, second_key = jax.random.split(key, 2)
    shape = (MW, 2, FIELDS, LEV, MW)
    base = jax.random.normal(first_key, shape, jnp.float32)
    scales = jnp.exp(jax.random.uniform(second_key, (1, 1, FIELDS, LEV, 1), jnp.float32, 0.0, math.log(10.0)))
    return jnp.clip(base * scales, -40.0, 40.0)


def shuffle_block(block_key):
    return jax.random.permutation(block_key, MW // 32)


def draw_wave_map(key, part):
    block_width = MW // 32
    subkeys = jax.random.split(key, 32)
    shuffled = jax.vmap(shuffle_block)(subkeys).astype(jnp.int32)
    starts = jnp.arange(32, dtype=jnp.int32)[:, None] * block_width
    return (MW - 1 - (starts + shuffled)).reshape(MW).astype(jnp.int32)


def steps_of(stream_key, extent, cuts, smallest, top_value):
    def one(axis_at, parts):
        draws = jax.random.uniform(jax.random.fold_in(jax.random.fold_in(stream_key, 6), axis_at), (parts,), jnp.float32, smallest / len(cuts), top_value / len(cuts))
        return jnp.repeat(jnp.exp(draws), extent[axis_at] // parts).reshape((-1,) + (1,) * (len(extent) - axis_at - 1))

    factor_of = one(*cuts[0])
    for cut in cuts[1:]:
        factor_of = factor_of * one(*cut)
    return factor_of


def centred(rng, shape, deviation, most, pieces=(), held_as=jnp.bfloat16):
    drawn = jax.random.normal(rng, shape, jnp.float32) * deviation
    if len(pieces) > 0:
        drawn = steps_of(rng, shape, pieces, -0.22, 0.18) * drawn
    return jnp.clip(drawn, min=-most, max=most).astype(held_as)


def setup_inputs(seed: int = 0) -> dict:
    splits = jax.random.split(jax.random.key(seed), 5)
    right_side = draw_right_side(jax.random.fold_in(splits[4], 71), 0)
    legendre = centred(splits[1], (MW, MW, NLAT), MW ** -0.5, 0.25, ((0, 64),))
    wave_map = draw_wave_map(jax.random.fold_in(splits[4], 71), 0)
    obs_weight = jnp.clip(jnp.exp(math.log(5.0) - 3.218876 * jax.random.uniform(splits[3], (NLAT, NLON), jnp.float32) ** steps_of(splits[3], (NLAT, NLON), ((0, 64),), -0.2, 0.2)), 0.2, 5.0)
    return {"right_side": right_side, "legendre": legendre, "wave_map": wave_map, "obs_weight": obs_weight}


def triangle_of(own_waves, degrees):
    return (jnp.arange(degrees, dtype=jnp.int32)[None, :] >= own_waves[:, None]).astype(jnp.float32)

def fourier_of(wave_map, lon_count):
    longitude = jnp.arange(lon_count, dtype=jnp.int32)
    phase_int = wave_map[:, None].astype(jnp.int32) * longitude[None, :] % lon_count
    angles = phase_int.astype(jnp.float32) * (2.0 * math.pi / lon_count)
    norm_factor = 1.0 / math.sqrt(wave_map.shape[0])
    return (jnp.stack([jnp.cos(angles), -jnp.sin(angles)], axis=1) * norm_factor).astype(jnp.bfloat16)

def operate(vector, legendre, fourier_table, triangle, obs_weight):
    masked_bf = (vector * triangle[:, None, None, None, :]).astype(jnp.bfloat16)
    coeffs = lax.dot_general(masked_bf, legendre, (((4,), (1,)), ((0,), (0,))), preferred_element_type=jnp.float32).astype(jnp.bfloat16)
    grid_vals = lax.dot_general(coeffs, fourier_table, (((0, 1), (0, 1)), ((), ())), preferred_element_type=jnp.float32)
    weighted = (grid_vals * obs_weight).astype(jnp.bfloat16)
    returned = lax.dot_general(fourier_table, weighted, (((2,), (3,)), ((), ())), preferred_element_type=jnp.float32).astype(jnp.bfloat16)
    adjoint = lax.dot_general(returned, legendre, (((4,), (2,)), ((0,), (0,))), preferred_element_type=jnp.float32)
    return vector + triangle[:, None, None, None, :] * adjoint

def reference(right_side, legendre, wave_map, obs_weight):
    triangle = triangle_of(wave_map, right_side.shape[4])
    fourier_table = fourier_of(wave_map, obs_weight.shape[1])
    residual = right_side * triangle[:, None, None, None, :]
    direction = residual
    solution = jnp.zeros_like(residual)
    norm_now = jnp.sum(residual * residual)
    for iteration in range(ITERS):
        image_vec = operate(direction, legendre, fourier_table, triangle, obs_weight)
        step_length = norm_now / jnp.sum(direction * image_vec)
        solution = solution + step_length * direction
        residual = residual - step_length * image_vec
        norm_next = jnp.sum(residual * residual)
        direction = residual + norm_next / norm_now * direction
        norm_now = norm_next
    return (solution, residual)
```

```python
import math

import jax
import jax.numpy as jnp
import numpy as np
from jax import lax
from jax.experimental import pallas as pl
from jax.experimental.pallas import tpu as pltpu
from jax.sharding import PartitionSpec as P

ITERS = 3
BANDS = 64
FIELD = 4
SLOTS = 10
LEV = 12
MW = 640
NLON = 1280
LANES = 128
LATBLOCKS = 5
WORKERS = LEV * LATBLOCKS
MSG = 2 * SLOTS
OWN_ROWS = SLOTS * 2 * LEV * LATBLOCKS
HALF = NLON // 2
KPAD = 656
WCOL = 704
WROW = 16
WSRC = 14
MESH = pl.DeviceIdType.MESH


def small_tables():
    k = np.arange(KPAD)
    keep = (k <= HALF).astype(np.float64)
    out = []
    for count, step in ((MW // 32, 32), (32, 1)):
        phase = (np.arange(count)[:, None] * step * k[None, :]) % NLON
        angle = phase * (2.0 * math.pi / NLON)
        out.append((np.cos(angle) * keep).astype(np.float32))
        out.append((np.sin(angle) * keep).astype(np.float32))
    return out


def spread_offset(i):
    half = lax.div(i + 1, 2)
    return jnp.where(lax.rem(i, 2) == 1, half, BANDS - half)


def kernel(
    rhs, leg_hbm, tri, wave_row, wts, ca, sa, cb, sb,
    x_ref, r_ref,
    leg, p_ref, s_ref, z_ref, stage, fsend, frecv, gsend, grecv,
    tc, ts, ckm, skm, cmk, smk, wa, wb, wrecv, a1s, a1r, a2s, a2r, scal,
    leg_sem, f_ssem, f_rsem, g_ssem, g_rsem, w_ssem, w_rsem, a1_ssem, a1_rsem, a2_ssem, a2_rsem,
):
    me = lax.axis_index("band")
    fld = lax.axis_index("field")
    zz = lax.div(me, 8)
    yy = lax.rem(lax.div(me, 2), 4)
    core = lax.rem(me, 2)
    worker = me < WORKERS

    wrecv[pl.ds((WSRC - 1) * WROW, WROW), :] = jnp.zeros((WROW, 2 * WCOL), jnp.bfloat16)

    barrier = pltpu.get_barrier_semaphore()

    def greet_band(i, c):
        pl.semaphore_signal(barrier, inc=1, device_id={"band": lax.rem(me + i, BANDS)}, device_id_type=MESH)
        return c

    def greet_field(i, c):
        f2 = lax.rem(fld + 1 + lax.div(i, 4), FIELD)
        b2 = zz * 8 + lax.rem(i, 4) * 2 + core
        pl.semaphore_signal(barrier, inc=1, device_id={"band": b2, "field": f2}, device_id_type=MESH)
        return c

    lax.fori_loop(1, BANDS, greet_band, 0)
    lax.fori_loop(0, 12, greet_field, 0)

    def leg_copy(s):
        return pltpu.make_async_copy(leg_hbm.at[s], leg.at[s], leg_sem.at[s])

    def start_leg(s, c):
        leg_copy(s).start()
        return c

    lax.fori_loop(0, SLOTS, start_leg, 0)

    def mask_slot(s, c):
        for j in range(LATBLOCKS):
            rows = pl.ds(s * 120 + j, 24, stride=5)
            r_ref[rows, :] = rhs[rows, :] * tri[s, :, 128 * j : 128 * j + 128]
        return c

    lax.fori_loop(0, SLOTS, mask_slot, 0)
    r0 = r_ref[...]
    scal[0:1, :] = jnp.sum(r0 * r0, axis=0, keepdims=True)
    scal[1:2, :] = jnp.ones((1, LANES), jnp.float32)
    scal[2:3, :] = jnp.ones((1, LANES), jnp.float32)
    x_ref[...] = jnp.zeros_like(r0)
    p_ref[...] = jnp.zeros_like(r0)
    s_ref[...] = jnp.zeros_like(r0)

    pl.semaphore_wait(barrier, BANDS - 1 + 12)

    lat0 = me * SLOTS
    blk_lo = lax.div(lat0, LANES)
    blk_hi = lax.div(lat0 + SLOTS - 1, LANES)

    def first_src(j):
        return lax.div(j * LANES, SLOTS)

    def w_dst(j):
        return wrecv.at[pl.ds((me - first_src(j)) * WROW, WROW)]

    def send_weights(j):
        def one(i, c):
            g = j * LEV + i

            @pl.when(g != me)
            def _():
                pltpu.make_async_remote_copy(
                    wts, w_dst(j), w_ssem, w_rsem, device_id={"band": g}, device_id_type=MESH
                ).start()

            @pl.when(g == me)
            def _():
                pltpu.make_async_copy(wts, w_dst(j), w_rsem).start()

            return c

        lax.fori_loop(0, LEV, one, 0)

    send_weights(blk_lo)

    @pl.when(blk_hi != blk_lo)
    def _():
        send_weights(blk_hi)

    my_block = lax.div(me, LEV)

    def iteration(it, carry):
        def forward(s, c):
            @pl.when(it == 0)
            def _():
                leg_copy(s).wait()

            base = s * 120
            vec = jnp.concatenate(
                [r_ref[pl.ds(base + j, 24, stride=5), :] for j in range(LATBLOCKS)], axis=1
            ).astype(jnp.bfloat16)
            out = jnp.dot(vec, leg[s], preferred_element_type=jnp.float32)
            for j in range(LATBLOCKS):
                for cc in range(2):
                    stage[pl.ds(j * 240 + 2 * s + cc, LEV, stride=MSG), :] = out[
                        LEV * cc : LEV * cc + LEV, 128 * j : 128 * j + 128
                    ]
            return c

        lax.fori_loop(0, SLOTS, forward, 0)
        fsend[...] = stage[0:OWN_ROWS, :].astype(jnp.bfloat16)

        def f_block(g):
            return fsend.at[pl.ds(pl.multiple_of(g * MSG, 4), MSG)]

        f_dst = frecv.at[it, pl.ds(pl.multiple_of(me * MSG, 4), MSG)]

        @pl.when(worker)
        def _():
            pltpu.make_async_copy(f_block(me), f_dst, f_rsem.at[it]).start()

        def f_go(i, c):
            g = lax.rem(me + spread_offset(i), BANDS)

            @pl.when(g < WORKERS)
            def _():
                pltpu.make_async_remote_copy(
                    f_block(g), f_dst, f_ssem, f_rsem.at[it], device_id={"band": g}, device_id_type=MESH
                ).start()

            return c

        lax.fori_loop(1, BANDS, f_go, 0)

        @pl.when(it == 0)
        def _():
            norm = 1.0 / math.sqrt(MW)
            for a in range(MW // 32):
                cosa, sina = ca[a : a + 1, :], sa[a : a + 1, :]
                tc[32 * a : 32 * a + 32, :] = ((cosa * cb[...] - sina * sb[...]) * norm).astype(jnp.bfloat16)
                ts[32 * a : 32 * a + 32, :] = ((sina * cb[...] + cosa * sb[...]) * -norm).astype(jnp.bfloat16)
            pick = (
                lax.broadcasted_iota(jnp.int32, (MW, MW), 0) == wave_row[...]
            ).astype(jnp.float32).astype(jnp.bfloat16)
            contract = (((0,), (0,)), ((), ()))
            for src, km, mk in ((tc, ckm, cmk), (ts, skm, smk)):
                km[...] = lax.dot_general(
                    src[...], pick, contract, preferred_element_type=jnp.float32
                ).astype(jnp.bfloat16)
                mk[...] = lax.dot_general(
                    pick, src[...], contract, preferred_element_type=jnp.float32
                ).astype(jnp.bfloat16)

        @pl.when(jnp.logical_and(it == 0, worker))
        def _():
            edge = jnp.logical_or(my_block == 0, my_block == LATBLOCKS - 1)

            @pl.when(edge)
            def _():
                part13 = wrecv.at[pl.ds(0, 13 * WROW)]
                pltpu.make_async_copy(part13, part13, w_rsem).wait()

            @pl.when(jnp.logical_not(edge))
            def _():
                pltpu.make_async_copy(wrecv, wrecv, w_rsem).wait()

            row = lax.broadcasted_iota(jnp.int32, (WSRC * WROW, LANES), 0)
            lat = lax.broadcasted_iota(jnp.int32, (WSRC * WROW, LANES), 1)
            src_lat = (first_src(my_block) + row // WROW) * SLOTS + row % WROW
            hit = jnp.logical_and(row % WROW < SLOTS, src_lat - my_block * LANES == lat)
            spot = hit.astype(jnp.float32).astype(jnp.bfloat16)
            turned = lax.dot_general(
                wrecv[...], spot, (((0,), (0,)), ((), ())), preferred_element_type=jnp.float32
            )
            wa[...] = turned[0:KPAD]
            wb[...] = turned[WCOL : WCOL + KPAD]

        scal[3:4, :] = jnp.zeros((1, LANES), jnp.float32)

        @pl.when(worker)
        def _():
            pltpu.make_async_copy(frecv.at[it], frecv.at[it], f_rsem.at[it]).wait()
            stage[...] = frecv[it].astype(jnp.float32)
            even_in = stage[pl.ds(0, MW, stride=2), :].astype(jnp.bfloat16)
            odd_in = stage[pl.ds(1, MW, stride=2), :].astype(jnp.bfloat16)
            cg = jnp.dot(ckm[...], even_in, preferred_element_type=jnp.float32)
            sg = jnp.dot(skm[...], odd_in, preferred_element_type=jnp.float32)
            even = wa[...] * cg + wb[...] * sg
            odd = wb[...] * cg + wa[...] * sg
            scal[3:4, :] = jnp.sum(cg * even + sg * odd, axis=0, keepdims=True)
            stage[pl.ds(0, MW, stride=2), :] = jnp.dot(
                cmk[...], even.astype(jnp.bfloat16), preferred_element_type=jnp.float32
            )
            stage[pl.ds(1, MW, stride=2), :] = jnp.dot(
                smk[...], odd.astype(jnp.bfloat16), preferred_element_type=jnp.float32
            )
            gsend[...] = stage[...].astype(jnp.bfloat16)

            def g_block(d):
                return gsend.at[pl.ds(pl.multiple_of(d * MSG, 4), MSG)]

            g_dst = grecv.at[it, pl.ds(pl.multiple_of(me * MSG, 4), MSG)]
            pltpu.make_async_copy(g_block(me), g_dst, g_rsem.at[it]).start()

            def g_go(i, c):
                d = lax.rem(me + spread_offset(i), BANDS)
                pltpu.make_async_remote_copy(
                    g_block(d), g_dst, g_ssem, g_rsem.at[it], device_id={"band": d}, device_id_type=MESH
                ).start()
                return c

            lax.fori_loop(1, BANDS, g_go, 0)

        pair = jnp.concatenate([scal[0:1, :], scal[3:4, :]], axis=0)
        own1 = zz * 2 + core
        own2 = fld * 4 + yy
        a1s[it] = pair
        a1r[it, own1] = pair

        def a1_go(i, c):
            o = lax.rem(own1 + i, 16)
            b2 = lax.div(o, 2) * 8 + yy * 2 + lax.rem(o, 2)
            pltpu.make_async_remote_copy(
                a1s.at[it], a1r.at[it, own1], a1_ssem.at[it], a1_rsem.at[it],
                device_id={"band": b2}, device_id_type=MESH,
            ).start()
            return c

        lax.fori_loop(1, 16, a1_go, 0)
        fifteen1 = a1r.at[it, pl.ds(0, 15)]
        pltpu.make_async_copy(fifteen1, fifteen1, a1_rsem.at[it]).wait()
        total1 = jnp.sum(a1r[it], axis=0)
        a2s[it] = total1
        a2r[it, own2] = total1

        def a2_go(i, c):
            o = lax.rem(own2 + i, 16)
            b2 = zz * 8 + lax.rem(o, 4) * 2 + core
            pltpu.make_async_remote_copy(
                a2s.at[it], a2r.at[it, own2], a2_ssem.at[it], a2_rsem.at[it],
                device_id={"band": b2, "field": lax.div(o, 4)}, device_id_type=MESH,
            ).start()
            return c

        lax.fori_loop(1, 16, a2_go, 0)

        pltpu.make_async_copy(grecv.at[it], grecv.at[it], g_rsem.at[it]).wait()
        stage[0:OWN_ROWS, :] = grecv[it].astype(jnp.float32)

        def backward(s, c):
            vec = jnp.concatenate(
                [
                    jnp.concatenate(
                        [stage[pl.ds(j * 240 + 2 * s + cc, LEV, stride=MSG), :] for cc in range(2)], axis=0
                    )
                    for j in range(LATBLOCKS)
                ],
                axis=1,
            ).astype(jnp.bfloat16)
            out = lax.dot_general(
                vec, leg[s], (((1,), (1,)), ((), ())), preferred_element_type=jnp.float32
            )
            out = out * tri[s]
            base = s * 120
            for j in range(LATBLOCKS):
                rows = pl.ds(base + j, 24, stride=5)
                z_ref[rows, :] = r_ref[rows, :] + out[:, 128 * j : 128 * j + 128]
            return c

        lax.fori_loop(0, SLOTS, backward, 0)

        fifteen2 = a2r.at[it, pl.ds(0, 15)]
        pltpu.make_async_copy(fifteen2, fifteen2, a2_rsem.at[it]).wait()
        total2 = jnp.sum(jnp.sum(a2r[it], axis=0), axis=1, keepdims=True)
        rr = jnp.broadcast_to(total2[0:1, :], (1, LANES))
        product = jnp.broadcast_to(total2[0:1, :] + total2[1:2, :], (1, LANES))
        first = jnp.where(it == 0, 0.0, 1.0)
        beta = rr / scal[1:2, :] * first
        alpha = rr / (product - beta * rr / scal[2:3, :])
        scal[1:2, :] = rr
        scal[2:3, :] = alpha
        residual = r_ref[...]
        direction = residual + beta * p_ref[...]
        along = z_ref[...] + beta * s_ref[...]
        p_ref[...] = direction
        s_ref[...] = along
        x_ref[...] = x_ref[...] + alpha * direction
        residual = residual - alpha * along
        r_ref[...] = residual
        scal[0:1, :] = jnp.sum(residual * residual, axis=0, keepdims=True)

        most = frecv.at[0, pl.ds(0, 59 * MSG)]

        @pl.when(worker)
        def _():
            pltpu.make_async_copy(most, most, f_ssem).wait()
            sent = gsend.at[pl.ds(0, 63 * MSG)]
            pltpu.make_async_copy(sent, sent, g_ssem).wait()

        @pl.when(jnp.logical_not(worker))
        def _():
            sent = frecv.at[0, pl.ds(0, 60 * MSG)]
            pltpu.make_async_copy(sent, sent, f_ssem).wait()

        pltpu.make_async_copy(fifteen1, fifteen1, a1_ssem.at[it]).wait()
        pltpu.make_async_copy(fifteen2, fifteen2, a2_ssem.at[it]).wait()
        return carry

    lax.fori_loop(0, ITERS, iteration, 0)

    def w_sent(j):
        mine = jnp.logical_and(j * LEV <= me, me < j * LEV + LEV)

        @pl.when(mine)
        def _():
            part_ref = wrecv.at[pl.ds(0, 11 * WROW)]
            pltpu.make_async_copy(part_ref, part_ref, w_ssem).wait()

        @pl.when(jnp.logical_not(mine))
        def _():
            part_ref = wrecv.at[pl.ds(0, 12 * WROW)]
            pltpu.make_async_copy(part_ref, part_ref, w_ssem).wait()

    w_sent(blk_lo)

    @pl.when(blk_hi != blk_lo)
    def _():
        w_sent(blk_hi)


def on_device(right_side, legendre, wave_map, obs_weight):
    first_slot = lax.axis_index("band") * SLOTS
    own_waves = lax.dynamic_slice_in_dim(wave_map, first_slot, SLOTS)
    tri = (jnp.arange(MW, dtype=jnp.int32)[None, :] >= own_waves[:, None]).astype(jnp.float32)
    plus = obs_weight[:, : HALF + 1]
    mirror = jnp.pad(obs_weight[:, : HALF : -1], ((0, 0), (1, 1)))
    pad = ((0, WROW - SLOTS), (0, WCOL - HALF - 1))
    wts = jnp.concatenate([jnp.pad(plus + mirror, pad), jnp.pad(plus - mirror, pad)], axis=1).astype(jnp.bfloat16)
    tables = [jnp.asarray(t) for t in small_tables()]
    vmem = pl.BlockSpec(memory_space=pltpu.VMEM)
    f32, bf16 = jnp.float32, jnp.bfloat16
    dma = pltpu.SemaphoreType.DMA
    shape = jax.ShapeDtypeStruct((OWN_ROWS, LANES), f32)
    x, r = pl.pallas_call(
        kernel,
        out_shape=(shape, shape),
        in_specs=[vmem, pl.BlockSpec(memory_space=pl.ANY)] + [vmem] * 7,
        out_specs=(vmem, vmem),
        scratch_shapes=[
            pltpu.VMEM((SLOTS, MW, MW), bf16),
            pltpu.VMEM((OWN_ROWS, LANES), f32),
            pltpu.VMEM((OWN_ROWS, LANES), f32),
            pltpu.VMEM((OWN_ROWS, LANES), f32),
            pltpu.VMEM((BANDS * MSG, LANES), f32),
            pltpu.VMEM((OWN_ROWS, LANES), bf16),
            pltpu.VMEM((ITERS, BANDS * MSG, LANES), bf16),
            pltpu.VMEM((BANDS * MSG, LANES), bf16),
            pltpu.VMEM((ITERS, OWN_ROWS, LANES), bf16),
            pltpu.VMEM((MW, KPAD), bf16),
            pltpu.VMEM((MW, KPAD), bf16),
            pltpu.VMEM((KPAD, MW), bf16),
            pltpu.VMEM((KPAD, MW), bf16),
            pltpu.VMEM((MW, KPAD), bf16),
            pltpu.VMEM((MW, KPAD), bf16),
            pltpu.VMEM((KPAD, LANES), f32),
            pltpu.VMEM((KPAD, LANES), f32),
            pltpu.VMEM((WSRC * WROW, 2 * WCOL), bf16),
            pltpu.VMEM((ITERS, 2, LANES), f32),
            pltpu.VMEM((ITERS, 16, 2, LANES), f32),
            pltpu.VMEM((ITERS, 2, LANES), f32),
            pltpu.VMEM((ITERS, 16, 2, LANES), f32),
            pltpu.VMEM((8, LANES), f32),
            dma((SLOTS,)), dma(()), dma((ITERS,)), dma(()), dma((ITERS,)), dma(()), dma(()),
            dma((ITERS,)), dma((ITERS,)), dma((ITERS,)), dma((ITERS,)),
        ],
        compiler_params=pltpu.CompilerParams(
            collective_id=0, has_side_effects=True, vmem_limit_bytes=60 * 1024 * 1024
        ),
    )(
        right_side.reshape(OWN_ROWS, LANES), legendre, tri.reshape(SLOTS, 1, MW), wave_map.reshape(1, MW), wts, *tables
    )
    return x.reshape(right_side.shape), r.reshape(right_side.shape)


def solution(mesh):
    spec = P("band", None, "field", None, None)
    return jax.shard_map(
        on_device,
        mesh=mesh,
        in_specs=(spec, P("band", None, None), P(), P("band", None)),
        out_specs=(spec, spec),
        check_vma=False,
    )
```

```python
import math

import jax
import jax.numpy as jnp
import numpy as np
from jax import lax
from jax.experimental import pallas as pl
from jax.experimental.pallas import tpu as pltpu
from jax.sharding import PartitionSpec as P

ITERS = 3
BANDS = 64
FIELD = 4
SLOTS = 10
LEV = 12
MW = 640
NLON = 1280
LANES = 128
LATBLOCKS = 5
WORKERS = LEV * LATBLOCKS
MSG = 2 * SLOTS
OWN_ROWS = SLOTS * 2 * LEV * LATBLOCKS
HALF = NLON // 2
KPAD = 656
WROW = 16
WSRC = 14
MESH = pl.DeviceIdType.MESH


def small_tables():
    k = np.arange(KPAD)
    keep = (k <= HALF).astype(np.float64)
    out = []
    for count, step in ((MW // 32, 32), (32, 1)):
        phase = (np.arange(count)[:, None] * step * k[None, :]) % NLON
        angle = phase * (2.0 * math.pi / NLON)
        out.append((np.cos(angle) * keep).astype(np.float32))
        out.append((np.sin(angle) * keep).astype(np.float32))
    return out


def peer(i, zz, yy, core):
    zi, w = lax.div(i, 8), lax.rem(i, 8)
    yi = lax.div(w, 2)
    dz = jnp.where(lax.rem(zi, 2) == 0, 4 + lax.div(zi, 2), 4 - lax.div(zi + 1, 2))
    dy = jnp.where(lax.rem(yi, 2) == 0, 2 + lax.div(yi, 2), 2 - lax.div(yi + 1, 2))
    return lax.rem(zz + dz, 8) * 8 + lax.rem(yy + dy, 4) * 2 + lax.rem(core + lax.rem(w, 2), 2)


def kernel(
    rhs, leg_hbm, waves, wave_rows, obs, ca, sa, cb, sb,
    x_ref, p_ref, r_ref, s_ref, alpha_ref,
    leg, z_ref, stage, fsend, frecv, gsend, grecv,
    tc, ts, ckm, skm, cmk, smk, wa, wb, wsend, wrecv, a1s, a1r, a2s, a2r, scal,
    leg_sem, f_ssem, f_rsem, g_ssem, g_rsem, w_ssem, w_rsem, a1_ssem, a1_rsem, a2_ssem, a2_rsem,
):
    me = lax.axis_index("band")
    fld = lax.axis_index("field")
    zz = lax.div(me, 8)
    yy = lax.rem(lax.div(me, 2), 4)
    core = lax.rem(me, 2)
    worker = me < WORKERS

    wrecv[pl.ds((WSRC - 1) * WROW, WROW), :] = jnp.zeros((WROW, NLON), jnp.bfloat16)
    wsend[...] = jnp.concatenate(
        [obs[...], jnp.zeros((WROW - SLOTS, NLON), jnp.float32)], axis=0
    ).astype(jnp.bfloat16)

    barrier = pltpu.get_barrier_semaphore()

    def greet_band(i, c):
        pl.semaphore_signal(barrier, inc=1, device_id={"band": lax.rem(me + i, BANDS)}, device_id_type=MESH)
        return c

    def greet_field(i, c):
        f2 = lax.rem(fld + 1 + lax.div(i, 4), FIELD)
        b2 = zz * 8 + lax.rem(i, 4) * 2 + core
        pl.semaphore_signal(barrier, inc=1, device_id={"band": b2, "field": f2}, device_id_type=MESH)
        return c

    lax.fori_loop(1, BANDS, greet_band, 0)
    lax.fori_loop(0, 12, greet_field, 0)

    def leg_copy(s):
        return pltpu.make_async_copy(leg_hbm.at[s], leg.at[s], leg_sem.at[s])

    def start_leg(s, c):
        leg_copy(s).start()
        return c

    lax.fori_loop(0, SLOTS, start_leg, 0)

    degree = lax.broadcasted_iota(jnp.int32, (1, LANES), 1)

    def mask_slot(s, c):
        for j in range(LATBLOCKS):
            rows = pl.ds(s * 120 + j, 24, stride=5)
            r_ref[rows, :] = jnp.where(degree + 128 * j >= waves[me * SLOTS + s], rhs[rows, :], 0.0)
        return c

    lax.fori_loop(0, SLOTS, mask_slot, 0)
    r0 = r_ref[...]
    scal[0:1, :] = jnp.sum(r0 * r0, axis=0, keepdims=True)
    scal[1:2, :] = jnp.ones((1, LANES), jnp.float32)
    scal[2:3, :] = jnp.ones((1, LANES), jnp.float32)
    x_ref[...] = jnp.zeros_like(r0)
    p_ref[...] = jnp.zeros_like(r0)
    s_ref[...] = jnp.zeros_like(r0)

    pl.semaphore_wait(barrier, BANDS - 1 + 12)

    lat0 = me * SLOTS
    blk_lo = lax.div(lat0, LANES)
    blk_hi = lax.div(lat0 + SLOTS - 1, LANES)

    def first_src(j):
        return lax.div(j * LANES, SLOTS)

    def w_dst(j):
        return wrecv.at[pl.ds((me - first_src(j)) * WROW, WROW)]

    def send_weights(j):
        def one(i, c):
            g = j * LEV + i

            @pl.when(g != me)
            def _():
                pltpu.make_async_remote_copy(
                    wsend, w_dst(j), w_ssem, w_rsem, device_id={"band": g}, device_id_type=MESH
                ).start()

            @pl.when(g == me)
            def _():
                pltpu.make_async_copy(wsend, w_dst(j), w_rsem).start()

            return c

        lax.fori_loop(0, LEV, one, 0)

    send_weights(blk_lo)

    @pl.when(blk_hi != blk_lo)
    def _():
        send_weights(blk_hi)

    my_block = lax.div(me, LEV)

    def iteration(it, carry):
        def forward(s, c):
            @pl.when(it == 0)
            def _():
                leg_copy(s).wait()

            base = s * 120
            vec = jnp.concatenate(
                [r_ref[pl.ds(base + j, 24, stride=5), :] for j in range(LATBLOCKS)], axis=1
            ).astype(jnp.bfloat16)
            out = jnp.dot(vec, leg[s], preferred_element_type=jnp.float32)
            for j in range(LATBLOCKS):
                for cc in range(2):
                    stage[pl.ds(j * 240 + 2 * s + cc, LEV, stride=MSG), :] = out[
                        LEV * cc : LEV * cc + LEV, 128 * j : 128 * j + 128
                    ]
            return c

        lax.fori_loop(0, SLOTS, forward, 0)
        fsend[...] = stage[0:OWN_ROWS, :].astype(jnp.bfloat16)

        def f_block(g):
            return fsend.at[pl.ds(pl.multiple_of(g * MSG, 4), MSG)]

        f_dst = frecv.at[it, pl.ds(pl.multiple_of(me * MSG, 4), MSG)]

        @pl.when(worker)
        def _():
            pltpu.make_async_copy(f_block(me), f_dst, f_rsem.at[it]).start()

        def f_go(i, c):
            g = peer(i, zz, yy, core)

            @pl.when(jnp.logical_and(g < WORKERS, g != me))
            def _():
                pltpu.make_async_remote_copy(
                    f_block(g), f_dst, f_ssem, f_rsem.at[it], device_id={"band": g}, device_id_type=MESH
                ).start()

            return c

        lax.fori_loop(0, BANDS, f_go, 0)

        @pl.when(it == 0)
        def _():
            norm = 1.0 / math.sqrt(MW)
            for a in range(MW // 32):
                cosa, sina = ca[a : a + 1, :], sa[a : a + 1, :]
                tc[32 * a : 32 * a + 32, :] = ((cosa * cb[...] - sina * sb[...]) * norm).astype(jnp.bfloat16)
                ts[32 * a : 32 * a + 32, :] = ((sina * cb[...] + cosa * sb[...]) * -norm).astype(jnp.bfloat16)
            wave_row = jnp.concatenate([wave_rows[j : j + 1, :] for j in range(LATBLOCKS)], axis=1)
            pick = (
                lax.broadcasted_iota(jnp.int32, (MW, MW), 0) == wave_row
            ).astype(jnp.float32).astype(jnp.bfloat16)
            contract = (((0,), (0,)), ((), ()))
            for src, km, mk in ((tc, ckm, cmk), (ts, skm, smk)):
                km[...] = lax.dot_general(
                    src[...], pick, contract, preferred_element_type=jnp.float32
                ).astype(jnp.bfloat16)
                mk[...] = lax.dot_general(
                    pick, src[...], contract, preferred_element_type=jnp.float32
                ).astype(jnp.bfloat16)

        @pl.when(jnp.logical_and(it == 0, worker))
        def _():
            edge = jnp.logical_or(my_block == 0, my_block == LATBLOCKS - 1)

            @pl.when(edge)
            def _():
                part13 = wrecv.at[pl.ds(0, 13 * WROW)]
                pltpu.make_async_copy(part13, part13, w_rsem).wait()

            @pl.when(jnp.logical_not(edge))
            def _():
                pltpu.make_async_copy(wrecv, wrecv, w_rsem).wait()

            row = lax.broadcasted_iota(jnp.int32, (WSRC * WROW, LANES), 0)
            lat = lax.broadcasted_iota(jnp.int32, (WSRC * WROW, LANES), 1)
            src_lat = (first_src(my_block) + row // WROW) * SLOTS + row % WROW
            hit = jnp.logical_and(row % WROW < SLOTS, src_lat - my_block * LANES == lat)
            spot = hit.astype(jnp.float32).astype(jnp.bfloat16)
            turned = lax.dot_general(
                wrecv[...], spot, (((0,), (0,)), ((), ())), preferred_element_type=jnp.float32
            )
            k_row = lax.broadcasted_iota(jnp.int32, (KPAD, LANES), 0)
            plus = jnp.where(k_row <= HALF, turned[0:KPAD], 0.0)
            to_k = lax.broadcasted_iota(jnp.int32, (KPAD, HALF), 0)
            from_k = lax.broadcasted_iota(jnp.int32, (KPAD, HALF), 1)
            flip = jnp.logical_and(to_k + from_k == HALF, to_k < HALF).astype(jnp.float32).astype(jnp.bfloat16)
            mirror = jnp.dot(flip, turned[HALF:].astype(jnp.bfloat16), preferred_element_type=jnp.float32)
            wa[...] = plus + mirror
            wb[...] = plus - mirror

        scal[3:4, :] = jnp.zeros((1, LANES), jnp.float32)

        @pl.when(worker)
        def _():
            pltpu.make_async_copy(frecv.at[it], frecv.at[it], f_rsem.at[it]).wait()
            stage[...] = frecv[it].astype(jnp.float32)
            even_in = stage[pl.ds(0, MW, stride=2), :].astype(jnp.bfloat16)
            odd_in = stage[pl.ds(1, MW, stride=2), :].astype(jnp.bfloat16)
            cg = jnp.dot(ckm[...], even_in, preferred_element_type=jnp.float32)
            sg = jnp.dot(skm[...], odd_in, preferred_element_type=jnp.float32)
            even = wa[...] * cg + wb[...] * sg
            odd = wb[...] * cg + wa[...] * sg
            scal[3:4, :] = jnp.sum(cg * even + sg * odd, axis=0, keepdims=True)
            stage[pl.ds(0, MW, stride=2), :] = jnp.dot(
                cmk[...], even.astype(jnp.bfloat16), preferred_element_type=jnp.float32
            )
            stage[pl.ds(1, MW, stride=2), :] = jnp.dot(
                smk[...], odd.astype(jnp.bfloat16), preferred_element_type=jnp.float32
            )
            gsend[...] = stage[...].astype(jnp.bfloat16)

            def g_block(d):
                return gsend.at[pl.ds(pl.multiple_of(d * MSG, 4), MSG)]

            g_dst = grecv.at[it, pl.ds(pl.multiple_of(me * MSG, 4), MSG)]
            pltpu.make_async_copy(g_block(me), g_dst, g_rsem.at[it]).start()

            def g_go(i, c):
                d = peer(i, zz, yy, core)

                @pl.when(d != me)
                def _():
                    pltpu.make_async_remote_copy(
                        g_block(d), g_dst, g_ssem, g_rsem.at[it], device_id={"band": d}, device_id_type=MESH
                    ).start()

                return c

            lax.fori_loop(0, BANDS, g_go, 0)

        pair = jnp.concatenate([scal[0:1, :], scal[3:4, :]], axis=0)
        own1 = zz * 2 + core
        own2 = fld * 4 + yy
        a1s[it] = pair
        a1r[it, own1] = pair

        def a1_go(i, c):
            o = lax.rem(own1 + i, 16)
            b2 = lax.div(o, 2) * 8 + yy * 2 + lax.rem(o, 2)
            pltpu.make_async_remote_copy(
                a1s.at[it], a1r.at[it, own1], a1_ssem.at[it], a1_rsem.at[it],
                device_id={"band": b2}, device_id_type=MESH,
            ).start()
            return c

        lax.fori_loop(1, 16, a1_go, 0)
        fifteen1 = a1r.at[it, pl.ds(0, 15)]
        pltpu.make_async_copy(fifteen1, fifteen1, a1_rsem.at[it]).wait()
        total1 = jnp.sum(a1r[it], axis=0)
        a2s[it] = total1
        a2r[it, own2] = total1

        def a2_go(i, c):
            o = lax.rem(own2 + i, 16)
            b2 = zz * 8 + lax.rem(o, 4) * 2 + core
            pltpu.make_async_remote_copy(
                a2s.at[it], a2r.at[it, own2], a2_ssem.at[it], a2_rsem.at[it],
                device_id={"band": b2, "field": lax.div(o, 4)}, device_id_type=MESH,
            ).start()
            return c

        lax.fori_loop(1, 16, a2_go, 0)

        pltpu.make_async_copy(grecv.at[it], grecv.at[it], g_rsem.at[it]).wait()
        stage[0:OWN_ROWS, :] = grecv[it].astype(jnp.float32)

        def backward(s, c):
            vec = jnp.concatenate(
                [
                    jnp.concatenate(
                        [stage[pl.ds(j * 240 + 2 * s + cc, LEV, stride=MSG), :] for cc in range(2)], axis=0
                    )
                    for j in range(LATBLOCKS)
                ],
                axis=1,
            ).astype(jnp.bfloat16)
            out = lax.dot_general(
                vec, leg[s], (((1,), (1,)), ((), ())), preferred_element_type=jnp.float32
            )
            wave = waves[me * SLOTS + s]
            base = s * 120
            for j in range(LATBLOCKS):
                rows = pl.ds(base + j, 24, stride=5)
                adjoint = jnp.where(degree + 128 * j >= wave, out[:, 128 * j : 128 * j + 128], 0.0)
                z_ref[rows, :] = r_ref[rows, :] + adjoint
            return c

        lax.fori_loop(0, SLOTS, backward, 0)

        fifteen2 = a2r.at[it, pl.ds(0, 15)]
        pltpu.make_async_copy(fifteen2, fifteen2, a2_rsem.at[it]).wait()
        total2 = jnp.sum(jnp.sum(a2r[it], axis=0), axis=1, keepdims=True)
        rr = jnp.broadcast_to(total2[0:1, :], (1, LANES))
        product = jnp.broadcast_to(total2[0:1, :] + total2[1:2, :], (1, LANES))
        first = jnp.where(it == 0, 0.0, 1.0)
        beta = rr / scal[1:2, :] * first
        alpha = rr / (product - beta * rr / scal[2:3, :])
        scal[1:2, :] = rr
        scal[2:3, :] = alpha
        residual = r_ref[...]
        direction = residual + beta * p_ref[...]
        along = z_ref[...] + beta * s_ref[...]
        p_ref[...] = direction
        s_ref[...] = along

        @pl.when(it < ITERS - 1)
        def _():
            x_ref[...] = x_ref[...] + alpha * direction
            nxt = residual - alpha * along
            r_ref[...] = nxt
            scal[0:1, :] = jnp.sum(nxt * nxt, axis=0, keepdims=True)


        most = frecv.at[0, pl.ds(0, 59 * MSG)]

        @pl.when(worker)
        def _():
            pltpu.make_async_copy(most, most, f_ssem).wait()
            sent = gsend.at[pl.ds(0, 63 * MSG)]
            pltpu.make_async_copy(sent, sent, g_ssem).wait()

        @pl.when(jnp.logical_not(worker))
        def _():
            sent = frecv.at[0, pl.ds(0, 60 * MSG)]
            pltpu.make_async_copy(sent, sent, f_ssem).wait()

        pltpu.make_async_copy(fifteen1, fifteen1, a1_ssem.at[it]).wait()
        pltpu.make_async_copy(fifteen2, fifteen2, a2_ssem.at[it]).wait()
        return carry

    lax.fori_loop(0, ITERS, iteration, 0)
    alpha_ref[...] = scal[2:3, :]

    def w_sent(j):
        mine = jnp.logical_and(j * LEV <= me, me < j * LEV + LEV)

        @pl.when(mine)
        def _():
            part_ref = wrecv.at[pl.ds(0, 11 * WROW)]
            pltpu.make_async_copy(part_ref, part_ref, w_ssem).wait()

        @pl.when(jnp.logical_not(mine))
        def _():
            part_ref = wrecv.at[pl.ds(0, 12 * WROW)]
            pltpu.make_async_copy(part_ref, part_ref, w_ssem).wait()

    w_sent(blk_lo)

    @pl.when(blk_hi != blk_lo)
    def _():
        w_sent(blk_hi)


def on_device(right_side, legendre, wave_map, obs_weight):
    tables = [jnp.asarray(t) for t in small_tables()]
    vmem = pl.BlockSpec(memory_space=pltpu.VMEM)
    f32, bf16 = jnp.float32, jnp.bfloat16
    dma = pltpu.SemaphoreType.DMA
    shape = jax.ShapeDtypeStruct((OWN_ROWS, LANES), f32)
    x, p, r, s, alpha = pl.pallas_call(
        kernel,
        out_shape=(shape, shape, shape, shape, jax.ShapeDtypeStruct((1, LANES), f32)),
        in_specs=[vmem, pl.BlockSpec(memory_space=pl.ANY), pl.BlockSpec(memory_space=pltpu.SMEM)] + [vmem] * 6,
        out_specs=(vmem,) * 5,
        scratch_shapes=[
            pltpu.VMEM((SLOTS, MW, MW), bf16),
            pltpu.VMEM((OWN_ROWS, LANES), f32),
            pltpu.VMEM((BANDS * MSG, LANES), f32),
            pltpu.VMEM((OWN_ROWS, LANES), bf16),
            pltpu.VMEM((ITERS, BANDS * MSG, LANES), bf16),
            pltpu.VMEM((BANDS * MSG, LANES), bf16),
            pltpu.VMEM((ITERS, OWN_ROWS, LANES), bf16),
            pltpu.VMEM((MW, KPAD), bf16),
            pltpu.VMEM((MW, KPAD), bf16),
            pltpu.VMEM((KPAD, MW), bf16),
            pltpu.VMEM((KPAD, MW), bf16),
            pltpu.VMEM((MW, KPAD), bf16),
            pltpu.VMEM((MW, KPAD), bf16),
            pltpu.VMEM((KPAD, LANES), f32),
            pltpu.VMEM((KPAD, LANES), f32),
            pltpu.VMEM((WROW, NLON), bf16),
            pltpu.VMEM((WSRC * WROW, NLON), bf16),
            pltpu.VMEM((ITERS, 2, LANES), f32),
            pltpu.VMEM((ITERS, 16, 2, LANES), f32),
            pltpu.VMEM((ITERS, 2, LANES), f32),
            pltpu.VMEM((ITERS, 16, 2, LANES), f32),
            pltpu.VMEM((8, LANES), f32),
            dma((SLOTS,)), dma(()), dma((ITERS,)), dma(()), dma((ITERS,)), dma(()), dma(()),
            dma((ITERS,)), dma((ITERS,)), dma((ITERS,)), dma((ITERS,)),
        ],
        compiler_params=pltpu.CompilerParams(
            collective_id=0, has_side_effects=True, vmem_limit_bytes=58 * 1024 * 1024
        ),
    )(
        right_side.reshape(OWN_ROWS, LANES), legendre, wave_map, wave_map.reshape(LATBLOCKS, LANES), obs_weight, *tables
    )
    return (x + alpha * p).reshape(right_side.shape), (r - alpha * s).reshape(right_side.shape)


def solution(mesh):
    spec = P("band", None, "field", None, None)
    return jax.shard_map(
        on_device,
        mesh=mesh,
        in_specs=(spec, P("band", None, None), P(), P("band", None)),
        out_specs=(spec, spec),
        check_vma=False,
    )
```
